32 devices in a mesh: groups: 2 (over x), dp: 16 (over z, y, core).
Axes of the slice: x: 2, y: 2, z: 4, core: 2. Of those that a mesh axis runs over, the one named last changes fastest.
Arguments:
- inputs: bfloat16 [64, 128, 4096], P(('groups', 'dp')), parts along dimension 0, may hold values from -6 to 6
- outputs: bfloat16 [64, 128, 4096], P(('groups', 'dp')), parts along dimension 0, may hold values from -6 to 6
- lengths: int32 [64], P(('groups', 'dp')), parts along dimension 0, may hold values from 64 to 128
- labels: int32 [64], P(('groups', 'dp')), parts along dimension 0, may hold values from 0 to 13
- norm_gain: float32 [4096], replicated, may hold values from 0.1 to 1.9
- classifier: bfloat16 [4096, 14], replicated, may hold values from -0.09375 to 0.09375
- proj_in: bfloat16 [4096, 64], replicated, may hold values from -0.09375 to 0.09375
- proj_out: bfloat16 [4096, 128], replicated, may hold values from -0.09375 to 0.09375
- query_index: int32 [256], P('groups'), parts along dimension 0, may hold values from 0 to 31, as said below
- prior_fisher: float32 [16384, 8192], P('groups', 'dp'), parts along dimension 0, may hold values from -4 to 18, as said below
Outputs:
- influence: float32 [8192, 256], P('dp', 'groups'), parts along dimension 1
- scores: float32 [64, 128], P(('groups', 'dp')), parts along dimension 0
The draws below stay inside these ranges and needn't reach their ends.
There are 2 independent parts, one for each index of `groups`. The reference program is written for one: setup_inputs(seed, part) draws one part's arguments, and reference() takes and returns one part's arrays. A program takes and returns all parts, laid end to end along the dimension named above; an argument that names none is the same for every part. Nothing has to cross between parts.
Inputs may be any that keep to these rules, and one draw needn't show every extreme that they name: `query_index`: indices may repeat. `prior_fisher`: symmetric and positive definite.
All inputs are finite; a program needn't handle non-finite values.
Results may differ from the reference program's by a relative error of at most 0.0044.
Values may be sent and summed in bfloat16 or wider, within the bound.
A program may use at most 128 MiB of HBM per device.

```python
import jax
import jax.numpy as jnp
from jax import lax

D = 4096
CLASSES = 14
KI = 64
KO = 128
K = 8192
TOK_EX = 128
QUERIES = 128
ITERS = 4
EXAMPLES = 32


def draw_lengths(key, part):
    values = jax.random.randint(key, (EXAMPLES,), TOK_EX // 2, TOK_EX + 1)
    positions = jnp.arange(EXAMPLES)
    values = jnp.where(positions == 0, TOK_EX, values)
    values = jnp.where(positions == 1, TOK_EX // 2, values)
    return values.astype(jnp.int32)


def draw_labels(key, part):
    values = jax.random.randint(key, (EXAMPLES,), 0, CLASSES)
    positions = jnp.arange(EXAMPLES)
    values = jnp.where(positions == 0, CLASSES - 1, values)
    values = jnp.where(positions == 1, 0, values)
    return values.astype(jnp.int32)


def draw_query_index(key, part):
    values = jax.random.randint(key, (QUERIES,), 0, EXAMPLES)
    positions = jnp.arange(QUERIES)
    values = jnp.where(positions == 0, EXAMPLES - 1, values)
    values = jnp.where(positions == 1, 0, values)
    return values.astype(jnp.int32)


def draw_prior_fisher(key, part):
    noise_key = jax.random.fold_in(key, 101)
    diag_key = jax.random.fold_in(key, 202)
    spread = 0.35 / K ** 0.5
    noise = jnp.clip(jax.random.normal(noise_key, (K, K), jnp.float32), -6.0, 6.0)
    offdiag = (noise + noise.T) * (spread * 0.70710678)
    diag_values = 1.0 + jax.random.uniform(diag_key, (K,), jnp.float32)
    row_ids = lax_iota_rows()
    col_ids = lax_iota_cols()
    base = jnp.where(row_ids == col_ids, diag_values[None, :], offdiag)
    return base.astype(jnp.float32)


def lax_iota_rows():
    return jnp.arange(K, dtype=jnp.int32)[:, None]


def lax_iota_cols():
    return jnp.arange(K, dtype=jnp.int32)[None, :]


def block_scale(stream_key, extent, shards, low, largest):
    factor_of, own = 1.0, jax.random.fold_in(stream_key, 6)
    for dim, parts in shards:
        draws = jnp.exp(jax.random.uniform(jax.random.fold_in(own, dim), (parts,), jnp.float32, low / len(shards), largest / len(shards)))
        factor_of = factor_of * jnp.repeat(draws, extent[dim] // parts).reshape([-1 if axis == dim else 1 for axis in range(len(extent))])
    return factor_of


def bell_draw(own_key, shape, scale, reach, cuts=(), held_as=jnp.bfloat16):
    result = scale * jax.random.normal(own_key, shape, jnp.float32)
    if cuts:
        result = result * block_scale(own_key, shape, cuts, -0.22, 0.18)
    return jnp.clip(result, -reach, reach).astype(held_as)


def setup_inputs(seed: int = 0, part: int = 0) -> dict:
    key_of = jax.random.split(jax.random.key(seed), 11)
    own_keys = jax.random.split(jax.random.fold_in(key_of[10], part), 11)
    return {
        "inputs": bell_draw(own_keys[0], (EXAMPLES, TOK_EX, D), 1.0, 6.0, ((0, 16),)),
        "outputs": bell_draw(own_keys[1], (EXAMPLES, TOK_EX, D), 1.0, 6.0, ((0, 16),)),
        "lengths": draw_lengths(jax.random.fold_in(jax.random.fold_in(key_of[10], part), 71), part),
        "labels": draw_labels(jax.random.fold_in(jax.random.fold_in(key_of[10], part), 71), part),
        "norm_gain": jnp.clip(1.0 + 0.18 * jax.random.normal(key_of[4], (D,), jnp.float32), 0.1, 1.9),
        "classifier": bell_draw(key_of[5], (D, CLASSES), D ** -0.5, 0.09375),
        "proj_in": bell_draw(key_of[6], (D, KI), D ** -0.5, 0.09375),
        "proj_out": bell_draw(key_of[7], (D, KO), D ** -0.5, 0.09375),
        "query_index": draw_query_index(jax.random.fold_in(jax.random.fold_in(key_of[10], part), 71), part),
        "prior_fisher": draw_prior_fisher(jax.random.fold_in(jax.random.fold_in(key_of[10], part), 71), part),
    }


norm_eps = 1e-05
damp_share = 0.5
highest = lax.Precision.HIGHEST

def example_gradient(inputs_one, outputs_one, length_one, label_one, norm_gain, classifier, proj_in, proj_out):
    hidden = outputs_one.astype(jnp.float32)
    root_mean = jnp.sqrt(lax.optimization_barrier(jnp.mean(hidden * hidden, axis=-1, keepdims=True)) + norm_eps)
    positions = jnp.arange(TOK_EX, dtype=jnp.int32)
    live_mask = (positions < length_one).astype(jnp.float32)[:, None]
    length_float = length_one.astype(jnp.float32)
    normed = norm_gain * hidden / root_mean
    pooled = lax.optimization_barrier(jnp.sum(live_mask * normed, axis=0)) / length_float
    class_weight = classifier.astype(jnp.float32)
    logits = jnp.dot(pooled, class_weight, precision=highest)
    exponent = jnp.exp(logits)
    probs = exponent / jnp.sum(exponent)
    target = (jnp.arange(CLASSES, dtype=jnp.int32) == label_one).astype(jnp.float32)
    pooled_grad = jnp.dot(class_weight, probs - target, precision=highest)
    scaled = norm_gain * (live_mask / length_float) * pooled_grad[None, :]
    out_grad = scaled / root_mean - hidden * lax.optimization_barrier(jnp.sum(hidden * scaled, axis=-1, keepdims=True)) / (D * root_mean ** 3)
    grad_low = out_grad.astype(jnp.bfloat16)
    input_proj = jnp.dot(inputs_one.astype(jnp.float32), proj_in.astype(jnp.float32), precision=highest)
    grad_proj = jnp.dot(grad_low.astype(jnp.float32), proj_out.astype(jnp.float32), precision=highest)
    outer = jnp.dot(input_proj.T, grad_proj, precision=highest)
    return outer.reshape(KI * KO).astype(jnp.bfloat16)

def reference(inputs, outputs, lengths, labels, norm_gain, classifier, proj_in, proj_out, query_index, prior_fisher):

    def one_example(packed):
        return example_gradient(packed[0], packed[1], packed[2], packed[3], norm_gain, classifier, proj_in, proj_out)
    rows = lax.map(one_example, (inputs, outputs, lengths, labels))
    rows_float = rows.astype(jnp.float32)
    damping = damp_share * jnp.sum(rows_float * rows_float) / (EXAMPLES * EXAMPLES)
    fisher = jnp.dot(rows_float.T, rows_float, precision=highest) / EXAMPLES
    fisher = fisher + damping * prior_fisher
    queries = rows_float[query_index].T
    solved = jnp.zeros_like(queries)
    residual = queries
    direction = queries
    norm_now = lax.optimization_barrier(jnp.sum(residual * residual, axis=0))
    for step_index in range(ITERS):
        image = jnp.dot(fisher, direction, precision=highest)
        alpha = norm_now / lax.optimization_barrier(jnp.sum(direction * image, axis=0))
        solved = solved + alpha * direction
        residual = residual - alpha * image
        norm_next = lax.optimization_barrier(jnp.sum(residual * residual, axis=0))
        direction = residual + norm_next / norm_now * direction
        norm_now = norm_next
    scores = jnp.dot(rows_float, solved, precision=highest) / EXAMPLES
    return (solved, scores)
```

```python
import functools

import jax
import jax.numpy as jnp
from jax import lax
from jax.experimental import pallas as pl
from jax.experimental.pallas import tpu as pltpu
from jax.sharding import PartitionSpec as P

D = 4096
CLASSES = 14
ITERS = 4


norm_eps = 1e-05
damp_share = 0.5
highest = lax.Precision.HIGHEST


def project_rows(inputs, outputs, lengths, labels, norm_gain, classifier, proj_in, proj_out):
    ex_count = inputs.shape[0]
    tok_count = inputs.shape[1]
    hidden = outputs.astype(jnp.float32)
    root_mean = jnp.sqrt(jnp.mean(hidden * hidden, axis=-1, keepdims=True) + norm_eps)
    positions = jnp.arange(tok_count, dtype=jnp.int32)
    live_mask = (positions[None, :] < lengths[:, None]).astype(jnp.float32)[:, :, None]
    length_float = lengths.astype(jnp.float32)[:, None, None]
    normed = norm_gain * hidden / root_mean
    pooled = jnp.sum(live_mask * normed, axis=1) / length_float[:, 0]
    class_weight = classifier.astype(jnp.float32)
    logits = jnp.dot(pooled, class_weight, precision=highest)
    exponent = jnp.exp(logits)
    probs = exponent / jnp.sum(exponent, axis=-1, keepdims=True)
    target = (jnp.arange(CLASSES, dtype=jnp.int32)[None, :] == labels[:, None]).astype(jnp.float32)
    pooled_grad = lax.dot_general(
        probs - target, class_weight, (((1,), (1,)), ((), ())), precision=highest
    )
    scaled = norm_gain * (live_mask / length_float) * pooled_grad[:, None, :]
    out_grad = scaled / root_mean - hidden * jnp.sum(hidden * scaled, axis=-1, keepdims=True) / (
        D * root_mean**3
    )
    grad_low = out_grad.astype(jnp.bfloat16)
    input_proj = jnp.dot(
        inputs.reshape(ex_count * tok_count, D),
        proj_in,
        preferred_element_type=jnp.float32,
    )
    grad_proj = jnp.dot(
        grad_low.reshape(ex_count * tok_count, D),
        proj_out,
        preferred_element_type=jnp.float32,
    )
    input_proj = input_proj.reshape(ex_count, tok_count, -1)
    grad_proj = grad_proj.reshape(ex_count, tok_count, -1)
    outer = jnp.einsum("eta,etb->eab", input_proj, grad_proj, precision=highest)
    return outer.astype(jnp.bfloat16)


BASIS_SCALE = 0.125
STAGES = 4
BUFFERS = 4


def solve_kernel(
    devices,
    rows_ref,
    query_ref,
    prior_ref,
    influence_ref,
    scores_ref,
    rows_all,
    rows_wide,
    vectors,
    own_vectors,
    prior_low,
    staging,
    small,
    row_send,
    row_pass,
    row_recv,
    vec_send,
    vec_pass,
    vec_recv,
    small_send,
    small_recv,
    stage_sem,
):
    me = lax.axis_index("dp")
    chips = devices // 2
    chip = me // 2
    core = lax.rem(me, 2)
    sibling = chip * 2 + 1 - core
    own_count, feat_in, feat_out = rows_ref.shape
    total = own_count * devices
    width, piece = prior_ref.shape
    span = 4 * total
    groups_in = feat_in // devices

    def load(step):
        block = lax.rem(me + step, devices)
        return pltpu.make_async_copy(
            prior_ref.at[pl.ds(pl.multiple_of(block * piece, piece), piece)],
            staging.at[lax.rem(step, BUFFERS)],
            stage_sem.at[lax.rem(step, BUFFERS)],
        )

    for step in range(BUFFERS):
        load(step).start()

    barrier = pltpu.get_barrier_semaphore()

    def greet(step, carry):
        pl.semaphore_signal(
            barrier, inc=1, device_id={"dp": lax.rem(me + step, devices)}
        )
        return carry

    lax.fori_loop(1, devices, greet, 0)
    pl.semaphore_wait(barrier, devices - 1)

    def send(view, sem_out, sem_in, target):
        return pltpu.make_async_remote_copy(
            src_ref=view,
            dst_ref=view,
            send_sem=sem_out,
            recv_sem=sem_in,
            device_id={"dp": target},
        )

    def row_view(source):
        return rows_all.at[pl.ds(source * own_count, own_count)]

    def row_copy(source, sem_out, target):
        return send(row_view(source), sem_out, row_recv.at[source], target)

    def vec_copy(stage, source, sem_out, target):
        view = vectors.at[source, pl.ds(stage * total, total)]
        return send(view, sem_out, vec_recv.at[stage, source], target)

    def near(step):
        return lax.rem(chip + chips - step, chips) * 2 + core

    def far(step):
        return lax.rem(chip + chips - step, chips) * 2 + 1 - core

    def ahead(step):
        return lax.rem(chip + step, chips) * 2 + core

    def gather(copy, out_sems, pass_sems, use, state):
        copy(me, out_sems(0), sibling).start()

        def push(step, carry):
            copy(me, out_sems(step), ahead(step)).start()
            return carry

        lax.fori_loop(1, chips, push, 0)
        state = use(me, state)

        def take_near(step, carry):
            source = near(step)
            copy(source, out_sems(step), ahead(step)).wait_recv()
            copy(source, pass_sems(step), sibling).start()
            return use(source, carry)

        state = lax.fori_loop(1, chips, take_near, state)

        def take_far(step, carry):
            source = far(step)
            copy(source, out_sems(0), sibling).wait_recv()
            return use(source, carry)

        return lax.fori_loop(0, chips, take_far, state)

    def drain(copy, out_sems, pass_sems):
        copy(me, out_sems(0), sibling).wait_send()

        def finish(step, carry):
            copy(me, out_sems(step), ahead(step)).wait_send()
            copy(near(step), pass_sems(step), sibling).wait_send()
            return carry

        lax.fori_loop(1, chips, finish, 0)

    def small_copy(turn, step, source, target):
        return send(
            small.at[turn, source], small_send.at[turn, step], small_recv.at[turn, source], target
        )

    def small_push(turn):
        def push(step, carry):
            small_copy(turn, step, me, lax.rem(me + step, devices)).start()
            return carry

        lax.fori_loop(1, devices, push, 0)

    def small_sum(turn):
        def finish(step, carry):
            source = lax.rem(me + devices - step, devices)
            small_copy(turn, step, source, source).wait_recv()
            small_copy(turn, step, me, source).wait_send()
            return carry

        lax.fori_loop(1, devices, finish, 0)
        return jnp.sum(small[turn], axis=0)

    rows_all[pl.ds(me * own_count, own_count)] = rows_ref[...]
    row_sems = (row_copy, lambda step: row_send.at[step], lambda step: row_pass.at[step])

    def cast_first():
        load(0).wait()
        block = staging[0]
        row_ids = lax.broadcasted_iota(jnp.int32, (piece, piece), 0)
        col_ids = lax.broadcasted_iota(jnp.int32, (piece, piece), 1)
        on_diag = row_ids == col_ids
        diag = jnp.sum(jnp.where(on_diag, block, 0.0), axis=0, keepdims=True)
        prior_low[me] = jnp.where(on_diag, 0.0, block).astype(jnp.bfloat16)
        load(BUFFERS).start()
        return diag

    diag = cast_first()
    mean_diag = jnp.sum(diag) / width
    small[0, me] = jnp.full(small.shape[2:], mean_diag, jnp.float32)
    small_push(0)

    def cast(step, carry):
        load(step).wait()
        prior_low[lax.rem(me + step, devices)] = staging[lax.rem(step, BUFFERS)].astype(
            jnp.bfloat16
        )

        @pl.when(step + BUFFERS < devices)
        def _():
            load(step + BUFFERS).start()

        return carry

    def use_rows(source, step):
        @pl.when(step > 0)
        def _():
            cast(step, 0)

        return step + 1

    gather(*row_sems, use_rows, 0)

    def widen(step, carry):
        rows_wide[pl.ds(pl.multiple_of(step * feat_in, feat_in), feat_in)] = rows_all[
            step
        ].astype(jnp.float32)
        return carry

    lax.fori_loop(0, total, widen, 0)
    for index in range(feat_in):
        vectors[
            index // groups_in,
            0:total,
            (index % groups_in) * feat_out : (index % groups_in + 1) * feat_out,
        ] = rows_wide[pl.ds(index, total, stride=feat_in), :].astype(jnp.bfloat16)

    shift = small_sum(0)[0:1, 0:1]
    diag = diag - shift

    def partial(stage):
        def use(source, acc):
            return acc + jnp.dot(
                vectors[source, stage * total : (stage + 1) * total, :],
                prior_low[source],
                preferred_element_type=jnp.float32,
            )

        return use

    def next_vector(stage, acc):
        return BASIS_SCALE * (acc + diag * own_vectors[stage * total : (stage + 1) * total, :])

    zero = jnp.zeros((total, piece), jnp.float32)
    own_vectors[0:total, :] = vectors[me, 0:total, :].astype(jnp.float32)
    acc = lax.fori_loop(0, devices, partial(0), zero)
    for stage in range(1, STAGES):
        fresh = next_vector(stage - 1, acc)
        own_vectors[stage * total : (stage + 1) * total, :] = fresh
        vectors[me, stage * total : (stage + 1) * total, :] = fresh.astype(jnp.bfloat16)
        acc = gather(
            functools.partial(vec_copy, stage),
            lambda step, stage=stage: vec_send.at[stage, step],
            lambda step, stage=stage: vec_pass.at[stage, step],
            partial(stage),
            zero,
        )
    last = next_vector(STAGES - 1, acc)
    product = last * own_vectors[3 * total :, :]
    small[1, me] = lax.dot_general(
        jnp.ones((8, piece), jnp.float32),
        product,
        (((1,), (1,)), ((), ())),
        precision=highest,
        preferred_element_type=jnp.float32,
    )
    small_push(1)

    def add_gram(source, acc):
        block = vectors[source]
        return acc + lax.dot_general(
            block, block, (((1,), (1,)), ((), ())), preferred_element_type=jnp.float32
        )

    gram = lax.fori_loop(0, devices, add_gram, jnp.zeros((span, span), jnp.float32))

    row_ids = lax.broadcasted_iota(jnp.int32, (span, span), 0)
    col_ids = lax.broadcasted_iota(jnp.int32, (span, span), 1)
    trace = jnp.sum(
        jnp.sum(
            jnp.where((row_ids == col_ids) & (row_ids < total), gram, 0.0), axis=0, keepdims=True
        ),
        axis=1,
        keepdims=True,
    )
    damping = damp_share * trace / (total * total)
    lower = damping * shift
    raise_ = damping / BASIS_SCALE
    lanes = lax.broadcasted_iota(jnp.int32, (total, span), 1)
    start = (lanes == lax.broadcasted_iota(jnp.int32, (total, span), 0)).astype(jnp.float32)
    final_lanes = lanes >= 3 * total

    def shift_up(coeffs):
        return jnp.where(lanes >= total, pltpu.roll(coeffs, total, 1), 0.0)

    def dot32(left, right):
        return jnp.dot(left, right, precision=highest, preferred_element_type=jnp.float32)

    def inner(left, right):
        return jnp.sum(left * right, axis=1, keepdims=True)

    solved = jnp.zeros((total, span), jnp.float32)
    residual = start
    direction = start
    projected = dot32(start, gram)
    norm_now = inner(projected, residual)
    for step in range(ITERS):
        moved = shift_up(direction)
        image = (
            jnp.where(lanes < total, projected / total, 0.0) + lower * direction + raise_ * moved
        )
        energy = inner(projected, image)
        if step == ITERS - 1:
            tail = jnp.where(final_lanes, direction, 0.0)
            energy = energy + raise_ * inner(dot32(moved, gram), tail)
            sevenths = small_sum(1)[0:1, :]
            pick = (
                lax.broadcasted_iota(jnp.int32, (total, total), 0)
                == lax.broadcasted_iota(jnp.int32, (total, total), 1)
            )
            seventh = jnp.sum(jnp.where(pick, sevenths, 0.0), axis=1, keepdims=True)
            energy = energy + raise_ * seventh * inner(tail, tail)
        alpha = norm_now / energy
        solved = solved + alpha * direction
        if step < ITERS - 1:
            residual = residual - alpha * image
            pulled = dot32(residual, gram)
            norm_next = inner(pulled, residual)
            ratio = norm_next / norm_now
            direction = residual + ratio * direction
            projected = pulled + ratio * projected
            norm_now = norm_next

    queries = query_ref.shape[0]
    chosen = (
        query_ref[...] == lax.broadcasted_iota(jnp.int32, (queries, total), 1)
    ).astype(jnp.float32)
    picked = dot32(chosen, solved)
    influence_ref[...] = dot32(picked, own_vectors[...]).T
    own_ids = lax.broadcasted_iota(jnp.int32, (8, span), 0) + me * own_count
    own_rows = (
        (own_ids == lax.broadcasted_iota(jnp.int32, (8, span), 1))
        & (lax.broadcasted_iota(jnp.int32, (8, span), 0) < own_count)
    ).astype(jnp.float32)
    shares = dot32(own_rows, gram)
    scored = lax.dot_general(
        shares,
        picked,
        (((1,), (1,)), ((), ())),
        precision=highest,
        preferred_element_type=jnp.float32,
    )
    scores_ref[...] = scored[0:own_count, :] / total

    drain(*row_sems)
    for stage in range(1, STAGES):
        drain(
            functools.partial(vec_copy, stage),
            lambda step, stage=stage: vec_send.at[stage, step],
            lambda step, stage=stage: vec_pass.at[stage, step],
        )


def solve(own_rows, query_index, prior_fisher):
    devices = lax.axis_size("dp")
    own_count, feat_in, feat_out = own_rows.shape
    width, piece = prior_fisher.shape
    total = own_count * devices
    queries = query_index.shape[0]
    vmem = pl.BlockSpec(memory_space=pltpu.VMEM)
    dma = pltpu.SemaphoreType.DMA
    chips = devices // 2
    return pl.pallas_call(
        functools.partial(solve_kernel, devices),
        out_shape=(
            jax.ShapeDtypeStruct((piece, queries), jnp.float32),
            jax.ShapeDtypeStruct((own_count, queries), jnp.float32),
        ),
        in_specs=[vmem, vmem, pl.BlockSpec(memory_space=pl.ANY)],
        out_specs=(vmem, vmem),
        scratch_shapes=[
            pltpu.VMEM((total, feat_in, feat_out), jnp.bfloat16),
            pltpu.VMEM((total * feat_in, feat_out), jnp.float32),
            pltpu.VMEM((devices, 4 * total, piece), jnp.bfloat16),
            pltpu.VMEM((4 * total, piece), jnp.float32),
            pltpu.VMEM((devices, piece, piece), jnp.bfloat16),
            pltpu.VMEM((BUFFERS, piece, piece), jnp.float32),
            pltpu.VMEM((2, devices, 8, total), jnp.float32),
            dma((chips,)),
            dma((chips,)),
            dma((devices,)),
            dma((STAGES, chips)),
            dma((STAGES, chips)),
            dma((STAGES, devices)),
            dma((2, devices)),
            dma((2, devices)),
            dma((BUFFERS,)),
        ],
        compiler_params=pltpu.CompilerParams(
            collective_id=0, has_side_effects=True, vmem_limit_bytes=50 * 1024 * 1024
        ),
        name="solve",
    )(own_rows, query_index[:, None], prior_fisher)


def body(
    inputs,
    outputs,
    lengths,
    labels,
    norm_gain,
    classifier,
    proj_in,
    proj_out,
    query_index,
    prior_fisher,
):
    own_rows = project_rows(
        inputs, outputs, lengths, labels, norm_gain, classifier, proj_in, proj_out
    )
    return solve(own_rows, query_index, prior_fisher)


def solution(mesh):
    return jax.shard_map(
        body,
        mesh=mesh,
        in_specs=(
            P(("groups", "dp"), None, None),
            P(("groups", "dp"), None, None),
            P(("groups", "dp")),
            P(("groups", "dp")),
            P(),
            P(),
            P(),
            P(),
            P("groups"),
            P("groups", "dp"),
        ),
        out_specs=(P("dp", "groups"), P(("groups", "dp"), None)),
        check_vma=False,
    )
```

```python
import functools

import jax
import jax.numpy as jnp
from jax import lax
from jax.experimental import pallas as pl
from jax.experimental.pallas import tpu as pltpu
from jax.sharding import PartitionSpec as P

ITERS = 4


norm_eps = 1e-05
damp_share = 0.5
highest = lax.Precision.HIGHEST


BASIS_SCALE = 0.125
STAGES = 4
TOKENS = 16


def split_rows(value):
    high = value.astype(jnp.bfloat16)
    rest = value - high.astype(jnp.float32)
    middle = rest.astype(jnp.bfloat16)
    low = (rest - middle.astype(jnp.float32)).astype(jnp.bfloat16)
    return jnp.concatenate([high, middle, low], axis=0)


def join_rows(value):
    part = value.shape[0] // 3
    return value[0:part] + value[part : 2 * part] + value[2 * part :]


def dot32(left, right):
    return jnp.dot(left, right, precision=highest, preferred_element_type=jnp.float32)


def solve_kernel(
    devices,
    length_ref,
    label_ref,
    gain_ref,
    query_ref,
    inputs_ref,
    outputs_ref,
    classifier_ref,
    proj_in_ref,
    proj_out_ref,
    prior_ref,
    influence_ref,
    scores_ref,
    inputs_in,
    outputs_in,
    classifier_in,
    proj_in,
    proj_out,
    root_means,
    pooled_sums,
    scaled_rows,
    grads,
    rows_all,
    rows_wide,
    vectors,
    own_vectors,
    prior_low,
    staging,
    small,
    row_out,
    row_side,
    row_pass,
    row_recv,
    vec_out,
    vec_side,
    vec_pass,
    vec_recv,
    small_send,
    small_recv,
    stage_sem,
    input_sem,
):
    me = lax.axis_index("dp")
    columns = devices // 4
    column = me // 4
    row = lax.rem(me // 2, 2)
    core = lax.rem(me, 2)
    own_count, tokens, depth = inputs_ref.shape
    feat_in = proj_in_ref.shape[1]
    feat_out = proj_out_ref.shape[1]
    total = own_count * devices
    width, piece = prior_ref.shape
    span = 4 * total
    groups_in = feat_in // devices

    fetch = [
        pltpu.make_async_copy(source, target, input_sem.at[index])
        for index, (source, target) in enumerate(
            (
                (outputs_ref, outputs_in),
                (classifier_ref, classifier_in),
                (proj_out_ref, proj_out),
                (inputs_ref, inputs_in),
                (proj_in_ref, proj_in),
            )
        )
    ]
    for copy in fetch:
        copy.start()

    def load(step):
        block = lax.rem(me + step, devices)
        return pltpu.make_async_copy(
            prior_ref.at[pl.ds(pl.multiple_of(block * piece, piece), piece)],
            staging.at[step],
            stage_sem.at[step],
        )

    def load_start(step, carry):
        load(step).start()
        return carry

    lax.fori_loop(0, devices, load_start, 0)

    barrier = pltpu.get_barrier_semaphore()

    def greet(step, carry):
        pl.semaphore_signal(
            barrier, inc=1, device_id={"dp": lax.rem(me + step, devices)}
        )
        return carry

    lax.fori_loop(1, devices, greet, 0)

    blocks = tokens // TOKENS

    def live_of(example, start):
        positions = lax.broadcasted_iota(jnp.int32, (TOKENS, 1), 0) + start
        return (positions < length_ref[example]).astype(jnp.float32)

    scaled_rows[...] = jnp.zeros_like(scaled_rows)
    fetch[0].wait()
    for example in range(own_count):

        def pool(block, carry, example=example):
            start = pl.multiple_of(block * TOKENS, TOKENS)
            hidden = outputs_in[example, pl.ds(start, TOKENS), :].astype(jnp.float32)
            root_mean = jnp.sqrt(
                jnp.sum(hidden * hidden, axis=1, keepdims=True) / depth + norm_eps
            )
            root_means[example, pl.ds(start, TOKENS), :] = root_mean
            term = hidden * (live_of(example, start) / root_mean)
            pooled_sums[...] += jnp.sum(term.reshape(TOKENS // 8, 8, depth), axis=0)
            return carry

        pooled_sums[...] = jnp.zeros_like(pooled_sums)
        lax.fori_loop(0, blocks, pool, 0)
        scaled_rows[example : example + 1, :] = (
            gain_ref[...]
            * jnp.sum(pooled_sums[...], axis=0, keepdims=True)
            / length_ref[example].astype(jnp.float32)
        )

    fetch[1].wait()
    logits = join_rows(
        jnp.dot(
            split_rows(scaled_rows[...]), classifier_in[...], preferred_element_type=jnp.float32
        )
    )
    exponent = jnp.exp(logits)
    probs = exponent / jnp.sum(exponent, axis=1, keepdims=True)
    row_ids = lax.broadcasted_iota(jnp.int32, probs.shape, 0)
    class_ids = lax.broadcasted_iota(jnp.int32, probs.shape, 1)
    difference = probs
    for example in range(own_count):
        difference = difference - (
            (row_ids == example) & (class_ids == label_ref[example])
        ).astype(jnp.float32)
    pooled_grad = join_rows(
        lax.dot_general(
            split_rows(difference),
            classifier_in[...],
            (((1,), (1,)), ((), ())),
            preferred_element_type=jnp.float32,
        )
    )
    for example in range(own_count):
        scaled_rows[example : example + 1, :] = (
            gain_ref[...]
            * (1.0 / length_ref[example].astype(jnp.float32))
            * pooled_grad[example : example + 1, :]
        )

    for index in (2, 3, 4):
        fetch[index].wait()
    for example in range(own_count):

        def differentiate(block, carry, example=example):
            start = pl.multiple_of(block * TOKENS, TOKENS)
            hidden = outputs_in[example, pl.ds(start, TOKENS), :].astype(jnp.float32)
            root_mean = root_means[example, pl.ds(start, TOKENS), :]
            live = live_of(example, start)
            scaled = scaled_rows[example : example + 1, :]
            along = live * jnp.sum(hidden * scaled, axis=1, keepdims=True)
            along = along / (depth * root_mean * root_mean * root_mean)
            grads[pl.ds(start, TOKENS), :] = (
                scaled * (live / root_mean) - hidden * along
            ).astype(jnp.bfloat16)
            return carry

        lax.fori_loop(0, blocks, differentiate, 0)
        grad_proj = jnp.dot(grads[...], proj_out[...], preferred_element_type=jnp.float32)
        input_proj = jnp.dot(
            inputs_in[example], proj_in[...], preferred_element_type=jnp.float32
        )
        rows_all[me * own_count + example] = lax.dot_general(
            input_proj,
            grad_proj,
            (((0,), (0,)), ((), ())),
            precision=highest,
            preferred_element_type=jnp.float32,
        ).astype(jnp.bfloat16)

    pl.semaphore_wait(barrier, devices - 1)

    def send(view, sem_out, sem_in, target):
        return pltpu.make_async_remote_copy(
            src_ref=view,
            dst_ref=view,
            send_sem=sem_out,
            recv_sem=sem_in,
            device_id={"dp": target},
        )

    def row_view(source):
        return rows_all.at[pl.ds(source * own_count, own_count)]

    def row_copy(source, sem_out, target):
        return send(row_view(source), sem_out, row_recv.at[source], target)

    def vec_copy(stage, source, sem_out, target):
        view = vectors.at[source, pl.ds(stage * total, total)]
        return send(view, sem_out, vec_recv.at[stage, source], target)

    def device_at(step, other_row, other_core):
        at = lax.rem(column + columns + step, columns)
        return at * 4 + (1 - row if other_row else row) * 2 + (1 - core if other_core else core)

    side = device_at(0, True, False)
    sibling = device_at(0, False, True)

    def gather_start(copy, out, over, on):
        copy(me, over(0), side).start()

        def push(step, carry):
            copy(me, out(step), device_at(step, False, False)).start()
            return carry

        lax.fori_loop(1, columns, push, 0)
        copy(me, on(0), sibling).start()

    def gather(copy, out, over, on, use, state):
        state = use(me, state)

        def take_column(step, carry):
            source = device_at(-step, False, False)
            copy(source, on(step), sibling).wait_recv()
            copy(source, over(step), side).start()
            copy(source, on(step), sibling).start()
            return use(source, carry)

        state = lax.fori_loop(1, columns, take_column, state)

        def take_side(step, carry):
            source = device_at(-step, True, False)
            copy(source, on(columns + step), sibling).wait_recv()
            copy(source, on(columns + step), sibling).start()
            return use(source, carry)

        state = lax.fori_loop(0, columns, take_side, state)

        def take_core(step, carry):
            for other_row in (False, True):
                source = device_at(-step, other_row, True)
                copy(source, on(step), sibling).wait_recv()
                carry = use(source, carry)
            return carry

        return lax.fori_loop(0, columns, take_core, state)

    def drain(copy, out, over, on):
        def finish(step, carry):
            copy(device_at(-step, False, False), over(step), side).wait_send()
            copy(device_at(-step, False, False), on(step), sibling).wait_send()
            copy(device_at(-step, True, False), on(columns + step), sibling).wait_send()
            return carry

        lax.fori_loop(0, columns, finish, 0)

        def finish_column(step, carry):
            copy(me, out(step), device_at(step, False, False)).wait_send()
            return carry

        lax.fori_loop(1, columns, finish_column, 0)

    def small_copy(turn, step, source, target):
        return send(
            small.at[turn, source], small_send.at[turn, step], small_recv.at[turn, source], target
        )

    def small_push(turn):
        def push(step, carry):
            small_copy(turn, step, me, lax.rem(me + step, devices)).start()
            return carry

        lax.fori_loop(1, devices, push, 0)

    def small_sum(turn):
        def finish(step, carry):
            source = lax.rem(me + devices - step, devices)
            small_copy(turn, step, source, source).wait_recv()
            small_copy(turn, step, me, source).wait_send()
            return carry

        lax.fori_loop(1, devices, finish, 0)
        return jnp.sum(small[turn], axis=0)

    def sems(array, *at):
        return lambda step: array.at[(*at, step)]

    row_sems = (row_copy, sems(row_out), sems(row_side), sems(row_pass))
    gather_start(*row_sems)

    load(0).wait()
    block = staging[0]
    on_diag = lax.broadcasted_iota(jnp.int32, (piece, piece), 0) == lax.broadcasted_iota(
        jnp.int32, (piece, piece), 1
    )
    diag = jnp.sum(jnp.where(on_diag, block, 0.0), axis=0, keepdims=True)
    prior_low[me] = jnp.where(on_diag, 0.0, block).astype(jnp.bfloat16)
    small[0, me] = jnp.full(small.shape[2:], jnp.sum(diag) / width, jnp.float32)
    small_push(0)

    def cast(step, carry):
        load(step).wait()
        prior_low[lax.rem(me + step, devices)] = staging[step].astype(jnp.bfloat16)
        return carry

    def use_rows(source, step):
        @pl.when(step > 0)
        def _():
            cast(step, 0)

        return step + 1

    gather(*row_sems, use_rows, 0)

    def widen(step, carry):
        rows_wide[pl.ds(pl.multiple_of(step * feat_in, feat_in), feat_in)] = rows_all[
            step
        ].astype(jnp.float32)
        return carry

    lax.fori_loop(0, total, widen, 0)
    for index in range(feat_in):
        vectors[
            index // groups_in,
            0:total,
            (index % groups_in) * feat_out : (index % groups_in + 1) * feat_out,
        ] = rows_wide[pl.ds(index, total, stride=feat_in), :].astype(jnp.bfloat16)

    shift = small_sum(0)[0:1, 0:1]
    diag = diag - shift

    def partial(stage):
        def use(source, acc):
            return acc + jnp.dot(
                vectors[source, stage * total : (stage + 1) * total, :],
                prior_low[source],
                preferred_element_type=jnp.float32,
            )

        return use

    def next_vector(stage, acc):
        return BASIS_SCALE * (acc + diag * own_vectors[stage * total : (stage + 1) * total, :])

    def vec_sems(stage):
        return (
            functools.partial(vec_copy, stage),
            sems(vec_out, stage),
            sems(vec_side, stage),
            sems(vec_pass, stage),
        )

    zero = jnp.zeros((total, piece), jnp.float32)
    own_vectors[0:total, :] = vectors[me, 0:total, :].astype(jnp.float32)
    acc = lax.fori_loop(0, devices, partial(0), zero)
    for stage in range(1, STAGES):
        fresh = next_vector(stage - 1, acc)
        own_vectors[stage * total : (stage + 1) * total, :] = fresh
        vectors[me, stage * total : (stage + 1) * total, :] = fresh.astype(jnp.bfloat16)
        gather_start(*vec_sems(stage))
        acc = gather(*vec_sems(stage), partial(stage), zero)
    last = next_vector(STAGES - 1, acc)
    product = last * own_vectors[3 * total :, :]
    small[1, me] = lax.dot_general(
        jnp.ones((8, piece), jnp.float32),
        product,
        (((1,), (1,)), ((), ())),
        precision=highest,
        preferred_element_type=jnp.float32,
    )
    small_push(1)

    def add_gram(source, acc):
        block = vectors[source]
        return acc + lax.dot_general(
            block, block, (((1,), (1,)), ((), ())), preferred_element_type=jnp.float32
        )

    gram = lax.fori_loop(0, devices, add_gram, jnp.zeros((span, span), jnp.float32))

    row_ids = lax.broadcasted_iota(jnp.int32, (span, span), 0)
    col_ids = lax.broadcasted_iota(jnp.int32, (span, span), 1)
    trace = jnp.sum(
        jnp.sum(
            jnp.where((row_ids == col_ids) & (row_ids < total), gram, 0.0), axis=0, keepdims=True
        ),
        axis=1,
        keepdims=True,
    )
    damping = damp_share * trace / (total * total)
    lower = damping * shift
    raise_ = damping / BASIS_SCALE
    lanes = lax.broadcasted_iota(jnp.int32, (total, span), 1)
    start = (lanes == lax.broadcasted_iota(jnp.int32, (total, span), 0)).astype(jnp.float32)
    final_lanes = lanes >= 3 * total

    def shift_up(coeffs):
        return jnp.where(lanes >= total, pltpu.roll(coeffs, total, 1), 0.0)

    def inner(left, right):
        return jnp.sum(left * right, axis=1, keepdims=True)

    solved = jnp.zeros((total, span), jnp.float32)
    residual = start
    direction = start
    projected = dot32(start, gram)
    norm_now = inner(projected, residual)
    for step in range(ITERS):
        moved = shift_up(direction)
        image = (
            jnp.where(lanes < total, projected / total, 0.0) + lower * direction + raise_ * moved
        )
        energy = inner(projected, image)
        if step == ITERS - 1:
            tail = jnp.where(final_lanes, direction, 0.0)
            energy = energy + raise_ * inner(dot32(moved, gram), tail)
            sevenths = small_sum(1)[0:1, :]
            pick = (
                lax.broadcasted_iota(jnp.int32, (total, total), 0)
                == lax.broadcasted_iota(jnp.int32, (total, total), 1)
            )
            seventh = jnp.sum(jnp.where(pick, sevenths, 0.0), axis=1, keepdims=True)
            energy = energy + raise_ * seventh * inner(tail, tail)
        alpha = norm_now / energy
        solved = solved + alpha * direction
        if step < ITERS - 1:
            residual = residual - alpha * image
            pulled = dot32(residual, gram)
            norm_next = inner(pulled, residual)
            ratio = norm_next / norm_now
            direction = residual + ratio * direction
            projected = pulled + ratio * projected
            norm_now = norm_next

    queries = query_ref.shape[0]
    chosen = (
        query_ref[...] == lax.broadcasted_iota(jnp.int32, (queries, total), 1)
    ).astype(jnp.float32)
    picked = dot32(chosen, solved)
    influence_ref[...] = dot32(picked, own_vectors[...]).T
    own_ids = lax.broadcasted_iota(jnp.int32, (8, span), 0) + me * own_count
    own_rows = (
        (own_ids == lax.broadcasted_iota(jnp.int32, (8, span), 1))
        & (lax.broadcasted_iota(jnp.int32, (8, span), 0) < own_count)
    ).astype(jnp.float32)
    shares = dot32(own_rows, gram)
    scored = lax.dot_general(
        shares,
        picked,
        (((1,), (1,)), ((), ())),
        precision=highest,
        preferred_element_type=jnp.float32,
    )
    scores_ref[...] = scored[0:own_count, :] / total

    drain(*row_sems)
    for stage in range(1, STAGES):
        drain(*vec_sems(stage))


def body(
    inputs,
    outputs,
    lengths,
    labels,
    norm_gain,
    classifier,
    proj_in,
    proj_out,
    query_index,
    prior_fisher,
):
    devices = lax.axis_size("dp")
    own_count, tokens, depth = inputs.shape
    feat_in, feat_out = proj_in.shape[1], proj_out.shape[1]
    width, piece = prior_fisher.shape
    total = own_count * devices
    queries = query_index.shape[0]
    columns = devices // 4
    vmem = pl.BlockSpec(memory_space=pltpu.VMEM)
    smem = pl.BlockSpec(memory_space=pltpu.SMEM)
    hbm = pl.BlockSpec(memory_space=pl.ANY)
    dma = pltpu.SemaphoreType.DMA
    return pl.pallas_call(
        functools.partial(solve_kernel, devices),
        out_shape=(
            jax.ShapeDtypeStruct((piece, queries), jnp.float32),
            jax.ShapeDtypeStruct((own_count, queries), jnp.float32),
        ),
        in_specs=[smem, smem, vmem, vmem, hbm, hbm, hbm, hbm, hbm, hbm],
        out_specs=(vmem, vmem),
        scratch_shapes=[
            pltpu.VMEM(inputs.shape, jnp.bfloat16),
            pltpu.VMEM(outputs.shape, jnp.bfloat16),
            pltpu.VMEM(classifier.shape, jnp.bfloat16),
            pltpu.VMEM(proj_in.shape, jnp.bfloat16),
            pltpu.VMEM(proj_out.shape, jnp.bfloat16),
            pltpu.VMEM((own_count, tokens, 1), jnp.float32),
            pltpu.VMEM((8, depth), jnp.float32),
            pltpu.VMEM((8, depth), jnp.float32),
            pltpu.VMEM((tokens, depth), jnp.bfloat16),
            pltpu.VMEM((total, feat_in, feat_out), jnp.bfloat16),
            pltpu.VMEM((total * feat_in, feat_out), jnp.float32),
            pltpu.VMEM((devices, 4 * total, piece), jnp.bfloat16),
            pltpu.VMEM((4 * total, piece), jnp.float32),
            pltpu.VMEM((devices, piece, piece), jnp.bfloat16),
            pltpu.VMEM((devices, piece, piece), jnp.float32),
            pltpu.VMEM((2, devices, 8, total), jnp.float32),
            dma((columns,)),
            dma((columns,)),
            dma((2 * columns,)),
            dma((devices,)),
            dma((STAGES, columns)),
            dma((STAGES, columns)),
            dma((STAGES, 2 * columns)),
            dma((STAGES, devices)),
            dma((2, devices)),
            dma((2, devices)),
            dma((devices,)),
            dma((5,)),
        ],
        compiler_params=pltpu.CompilerParams(
            collective_id=0, has_side_effects=True, vmem_limit_bytes=56 * 1024 * 1024
        ),
        name="solve",
    )(
        lengths,
        labels,
        norm_gain[None],
        query_index[:, None],
        inputs,
        outputs,
        classifier,
        proj_in,
        proj_out,
        prior_fisher,
    )


def solution(mesh):
    return jax.shard_map(
        body,
        mesh=mesh,
        in_specs=(
            P(("groups", "dp"), None, None),
            P(("groups", "dp"), None, None),
            P(("groups", "dp")),
            P(("groups", "dp")),
            P(),
            P(),
            P(),
            P(),
            P("groups"),
            P("groups", "dp"),
        ),
        out_specs=(P("dp", "groups"), P(("groups", "dp"), None)),
        check_vma=False,
    )
```

```python
import functools

import jax
import jax.numpy as jnp
from jax import lax
from jax.experimental import pallas as pl
from jax.experimental.pallas import tpu as pltpu
from jax.sharding import PartitionSpec as P

ITERS = 4


norm_eps = 1e-05
damp_share = 0.5
highest = lax.Precision.HIGHEST


BASIS_SCALE = 0.125
STAGES = 4
TOKENS = 16


def split_rows(value):
    high = value.astype(jnp.bfloat16)
    rest = value - high.astype(jnp.float32)
    middle = rest.astype(jnp.bfloat16)
    low = (rest - middle.astype(jnp.float32)).astype(jnp.bfloat16)
    return jnp.concatenate([high, middle, low], axis=0)


def join_rows(value):
    part = value.shape[0] // 3
    return value[0:part] + value[part : 2 * part] + value[2 * part :]


def dot32(left, right):
    return jnp.dot(left, right, precision=highest, preferred_element_type=jnp.float32)


def solve_kernel(
    devices,
    length_ref,
    label_ref,
    gain_ref,
    inputs_ref,
    outputs_ref,
    classifier_ref,
    proj_in_ref,
    proj_out_ref,
    prior_ref,
    solved_ref,
    own_vectors,
    shares_ref,
    inputs_in,
    outputs_in,
    classifier_in,
    proj_in,
    proj_out,
    root_means,
    pooled_sums,
    scaled_rows,
    grads,
    rows_all,
    rows_wide,
    vectors,
    prior_low,
    staging,
    small,
    row_out,
    row_side,
    row_pass,
    row_recv,
    vec_out,
    vec_side,
    vec_pass,
    vec_recv,
    small_send,
    small_recv,
    stage_sem,
    input_sem,
):
    me = lax.axis_index("dp")
    columns = devices // 4
    column = me // 4
    row = lax.rem(me // 2, 2)
    core = lax.rem(me, 2)
    own_count, tokens, depth = inputs_ref.shape
    feat_in = proj_in_ref.shape[0]
    feat_out = proj_out_ref.shape[1]
    total = own_count * devices
    width, piece = prior_ref.shape
    span = 4 * total
    groups_in = feat_in // devices

    fetch = [
        pltpu.make_async_copy(source, target, input_sem.at[index])
        for index, (source, target) in enumerate(
            (
                (outputs_ref, outputs_in),
                (classifier_ref, classifier_in),
                (proj_out_ref, proj_out),
                (inputs_ref, inputs_in),
                (proj_in_ref, proj_in),
            )
        )
    ]
    for copy in fetch:
        copy.start()

    def load(step):
        block = lax.rem(me + step, devices)
        return pltpu.make_async_copy(
            prior_ref.at[pl.ds(pl.multiple_of(block * piece, piece), piece)],
            staging.at[step],
            stage_sem.at[step],
        )

    def load_start(step, carry):
        load(step).start()
        return carry

    lax.fori_loop(0, devices, load_start, 0)

    barrier = pltpu.get_barrier_semaphore()

    def greet(step, carry):
        pl.semaphore_signal(
            barrier, inc=1, device_id={"dp": lax.rem(me + step, devices)}
        )
        return carry

    lax.fori_loop(1, devices, greet, 0)

    blocks = tokens // TOKENS

    def live_of(example, start):
        positions = lax.broadcasted_iota(jnp.int32, (TOKENS, 1), 0) + start
        return (positions < length_ref[example]).astype(jnp.float32)

    scaled_rows[...] = jnp.zeros_like(scaled_rows)
    fetch[0].wait()
    for example in range(own_count):

        def pool(block, carry, example=example):
            start = pl.multiple_of(block * TOKENS, TOKENS)
            hidden = outputs_in[example, pl.ds(start, TOKENS), :].astype(jnp.float32)
            root_mean = jnp.sqrt(
                jnp.sum(hidden * hidden, axis=1, keepdims=True) / depth + norm_eps
            )
            root_means[example, pl.ds(start, TOKENS), :] = root_mean
            term = hidden * (live_of(example, start) / root_mean)
            pooled_sums[...] += jnp.sum(term.reshape(TOKENS // 8, 8, depth), axis=0)
            return carry

        pooled_sums[...] = jnp.zeros_like(pooled_sums)
        lax.fori_loop(0, blocks, pool, 0)
        scaled_rows[example : example + 1, :] = (
            gain_ref[...]
            * jnp.sum(pooled_sums[...], axis=0, keepdims=True)
            / length_ref[example].astype(jnp.float32)
        )

    fetch[1].wait()
    logits = join_rows(
        lax.dot_general(
            split_rows(scaled_rows[...]),
            classifier_in[...],
            (((1,), (1,)), ((), ())),
            preferred_element_type=jnp.float32,
        )
    )
    exponent = jnp.exp(logits)
    probs = exponent / jnp.sum(exponent, axis=1, keepdims=True)
    row_ids = lax.broadcasted_iota(jnp.int32, probs.shape, 0)
    class_ids = lax.broadcasted_iota(jnp.int32, probs.shape, 1)
    difference = probs
    for example in range(own_count):
        difference = difference - (
            (row_ids == example) & (class_ids == label_ref[example])
        ).astype(jnp.float32)
    pooled_grad = join_rows(
        jnp.dot(split_rows(difference), classifier_in[...], preferred_element_type=jnp.float32)
    )
    for example in range(own_count):
        scaled_rows[example : example + 1, :] = (
            gain_ref[...]
            * (1.0 / length_ref[example].astype(jnp.float32))
            * pooled_grad[example : example + 1, :]
        )

    for index in (2, 3, 4):
        fetch[index].wait()
    for example in range(own_count):

        def differentiate(block, carry, example=example):
            start = pl.multiple_of(block * TOKENS, TOKENS)
            hidden = outputs_in[example, pl.ds(start, TOKENS), :].astype(jnp.float32)
            root_mean = root_means[example, pl.ds(start, TOKENS), :]
            live = live_of(example, start)
            scaled = scaled_rows[example : example + 1, :]
            along = live * jnp.sum(hidden * scaled, axis=1, keepdims=True)
            along = along / (depth * root_mean * root_mean * root_mean)
            grads[pl.ds(start, TOKENS), :] = (
                scaled * (live / root_mean) - hidden * along
            ).astype(jnp.bfloat16)
            return carry

        lax.fori_loop(0, blocks, differentiate, 0)
        grad_proj = jnp.dot(grads[...], proj_out[...], preferred_element_type=jnp.float32)
        input_proj = lax.dot_general(
            proj_in[...],
            inputs_in[example],
            (((1,), (1,)), ((), ())),
            preferred_element_type=jnp.float32,
        )
        rows_all[me * own_count + example] = dot32(input_proj, grad_proj).astype(jnp.bfloat16)

    pl.semaphore_wait(barrier, devices - 1)

    def send(view, sem_out, sem_in, target):
        return pltpu.make_async_remote_copy(
            src_ref=view,
            dst_ref=view,
            send_sem=sem_out,
            recv_sem=sem_in,
            device_id={"dp": target},
        )

    def row_view(source):
        return rows_all.at[pl.ds(source * own_count, own_count)]

    def row_copy(source, sem_out, target):
        return send(row_view(source), sem_out, row_recv.at[source], target)

    def vec_copy(stage, source, sem_out, target):
        view = vectors.at[source, pl.ds(stage * total, total)]
        return send(view, sem_out, vec_recv.at[stage, source], target)

    def device_at(step, other_row, other_core):
        at = lax.rem(column + columns + step, columns)
        return at * 4 + (1 - row if other_row else row) * 2 + (1 - core if other_core else core)

    side = device_at(0, True, False)
    sibling = device_at(0, False, True)

    def gather_start(copy, out, over, on):
        copy(me, over(0), side).start()

        def push(step, carry):
            copy(me, out(step), device_at(step, False, False)).start()
            return carry

        lax.fori_loop(1, columns, push, 0)
        copy(me, on(0), sibling).start()

    def gather(copy, out, over, on, use, state):
        state = use(me, state)

        def take_column(step, carry):
            source = device_at(-step, False, False)
            copy(source, on(step), sibling).wait_recv()
            copy(source, over(step), side).start()
            copy(source, on(step), sibling).start()
            return use(source, carry)

        state = lax.fori_loop(1, columns, take_column, state)

        def take_side(step, carry):
            source = device_at(-step, True, False)
            copy(source, on(columns + step), sibling).wait_recv()
            copy(source, on(columns + step), sibling).start()
            return use(source, carry)

        state = lax.fori_loop(0, columns, take_side, state)

        def take_core(step, carry):
            for other_row in (False, True):
                source = device_at(-step, other_row, True)
                copy(source, on(step), sibling).wait_recv()
                carry = use(source, carry)
            return carry

        return lax.fori_loop(0, columns, take_core, state)

    def drain(copy, out, over, on):
        def finish(step, carry):
            copy(device_at(-step, False, False), over(step), side).wait_send()
            copy(device_at(-step, False, False), on(step), sibling).wait_send()
            copy(device_at(-step, True, False), on(columns + step), sibling).wait_send()
            return carry

        lax.fori_loop(0, columns, finish, 0)

        def finish_column(step, carry):
            copy(me, out(step), device_at(step, False, False)).wait_send()
            return carry

        lax.fori_loop(1, columns, finish_column, 0)

    def small_copy(turn, step, source, target):
        return send(
            small.at[turn, source], small_send.at[turn, step], small_recv.at[turn, source], target
        )

    def small_push(turn):
        def push(step, carry):
            small_copy(turn, step, me, lax.rem(me + step, devices)).start()
            return carry

        lax.fori_loop(1, devices, push, 0)

    def small_sum(turn):
        def finish(step, carry):
            source = lax.rem(me + devices - step, devices)
            small_copy(turn, step, source, source).wait_recv()
            small_copy(turn, step, me, source).wait_send()
            return carry

        lax.fori_loop(1, devices, finish, 0)
        return jnp.sum(small[turn], axis=0)

    def sems(array, *at):
        return lambda step: array.at[(*at, step)]

    row_sems = (row_copy, sems(row_out), sems(row_side), sems(row_pass))
    gather_start(*row_sems)

    load(0).wait()
    block = staging[0]
    on_diag = lax.broadcasted_iota(jnp.int32, (piece, piece), 0) == lax.broadcasted_iota(
        jnp.int32, (piece, piece), 1
    )
    diag = jnp.sum(jnp.where(on_diag, block, 0.0), axis=0, keepdims=True)
    prior_low[me] = jnp.where(on_diag, 0.0, block).astype(jnp.bfloat16)
    small[0, me] = jnp.full(small.shape[2:], jnp.sum(diag) / width, jnp.float32)
    small_push(0)

    def cast(step, carry):
        load(step).wait()
        prior_low[lax.rem(me + step, devices)] = staging[step].astype(jnp.bfloat16)
        return carry

    def use_rows(source, step):
        @pl.when(step > 0)
        def _():
            cast(step, 0)

        return step + 1

    gather(*row_sems, use_rows, 0)

    def widen(step, carry):
        rows_wide[pl.ds(pl.multiple_of(step * feat_in, feat_in), feat_in)] = rows_all[
            step
        ].astype(jnp.float32)
        return carry

    lax.fori_loop(0, total, widen, 0)
    for index in range(feat_in):
        vectors[
            index // groups_in,
            0:total,
            (index % groups_in) * feat_out : (index % groups_in + 1) * feat_out,
        ] = rows_wide[pl.ds(index, total, stride=feat_in), :].astype(jnp.bfloat16)

    shift = small_sum(0)[0:1, 0:1]
    diag = diag - shift

    def partial(stage):
        def use(source, acc):
            return acc + jnp.dot(
                vectors[source, stage * total : (stage + 1) * total, :],
                prior_low[source],
                preferred_element_type=jnp.float32,
            )

        return use

    def next_vector(stage, acc):
        return BASIS_SCALE * (acc + diag * own_vectors[stage * total : (stage + 1) * total, :])

    def vec_sems(stage):
        return (
            functools.partial(vec_copy, stage),
            sems(vec_out, stage),
            sems(vec_side, stage),
            sems(vec_pass, stage),
        )

    zero = jnp.zeros((total, piece), jnp.float32)
    own_vectors[0:total, :] = vectors[me, 0:total, :].astype(jnp.float32)
    acc = lax.fori_loop(0, devices, partial(0), zero)
    for stage in range(1, STAGES):
        fresh = next_vector(stage - 1, acc)
        own_vectors[stage * total : (stage + 1) * total, :] = fresh
        vectors[me, stage * total : (stage + 1) * total, :] = fresh.astype(jnp.bfloat16)
        gather_start(*vec_sems(stage))
        acc = gather(*vec_sems(stage), partial(stage), zero)
    last = next_vector(STAGES - 1, acc)
    product = last * own_vectors[3 * total :, :]
    small[1, me] = lax.dot_general(
        jnp.ones((8, piece), jnp.float32),
        product,
        (((1,), (1,)), ((), ())),
        precision=highest,
        preferred_element_type=jnp.float32,
    )
    small_push(1)

    def add_gram(source, acc):
        block = vectors[source]
        return acc + lax.dot_general(
            block, block, (((1,), (1,)), ((), ())), preferred_element_type=jnp.float32
        )

    gram = lax.fori_loop(0, devices, add_gram, jnp.zeros((span, span), jnp.float32))

    row_ids = lax.broadcasted_iota(jnp.int32, (span, span), 0)
    col_ids = lax.broadcasted_iota(jnp.int32, (span, span), 1)
    trace = jnp.sum(
        jnp.sum(
            jnp.where((row_ids == col_ids) & (row_ids < total), gram, 0.0), axis=0, keepdims=True
        ),
        axis=1,
        keepdims=True,
    )
    damping = damp_share * trace / (total * total)
    lower = damping * shift
    raise_ = damping / BASIS_SCALE
    lanes = lax.broadcasted_iota(jnp.int32, (total, span), 1)
    start = (lanes == lax.broadcasted_iota(jnp.int32, (total, span), 0)).astype(jnp.float32)
    final_lanes = lanes >= 3 * total

    def shift_up(coeffs):
        return jnp.where(lanes >= total, pltpu.roll(coeffs, total, 1), 0.0)

    def inner(left, right):
        return jnp.sum(left * right, axis=1, keepdims=True)

    solved = jnp.zeros((total, span), jnp.float32)
    residual = start
    direction = start
    projected = dot32(start, gram)
    norm_now = inner(projected, residual)
    for step in range(ITERS):
        moved = shift_up(direction)
        image = (
            jnp.where(lanes < total, projected / total, 0.0) + lower * direction + raise_ * moved
        )
        energy = inner(projected, image)
        if step == ITERS - 1:
            tail = jnp.where(final_lanes, direction, 0.0)
            energy = energy + raise_ * inner(dot32(moved, gram), tail)
            sevenths = small_sum(1)[0:1, :]
            pick = (
                lax.broadcasted_iota(jnp.int32, (total, total), 0)
                == lax.broadcasted_iota(jnp.int32, (total, total), 1)
            )
            seventh = jnp.sum(jnp.where(pick, sevenths, 0.0), axis=1, keepdims=True)
            energy = energy + raise_ * seventh * inner(tail, tail)
        alpha = norm_now / energy
        solved = solved + alpha * direction
        if step < ITERS - 1:
            residual = residual - alpha * image
            pulled = dot32(residual, gram)
            norm_next = inner(pulled, residual)
            ratio = norm_next / norm_now
            direction = residual + ratio * direction
            projected = pulled + ratio * projected
            norm_now = norm_next

    solved_ref[...] = solved
    own_ids = lax.broadcasted_iota(jnp.int32, (8, span), 0) + me * own_count
    own_rows = (
        (own_ids == lax.broadcasted_iota(jnp.int32, (8, span), 1))
        & (lax.broadcasted_iota(jnp.int32, (8, span), 0) < own_count)
    ).astype(jnp.float32)
    shares_ref[...] = dot32(own_rows, gram) / total

    drain(*row_sems)
    for stage in range(1, STAGES):
        drain(*vec_sems(stage))


def finish_kernel(query_ref, solved_ref, own_vectors_ref, shares_ref, influence_ref, scores_ref):
    total = solved_ref.shape[0]
    queries = query_ref.shape[1]
    chosen = (
        lax.broadcasted_iota(jnp.int32, (total, queries), 0) == query_ref[...]
    ).astype(jnp.float32)
    picked = dot32(solved_ref[...].T, chosen)
    influence_ref[...] = dot32(own_vectors_ref[...].T, picked)
    scores_ref[...] = dot32(shares_ref[...], picked)[0 : scores_ref.shape[0], :]


def body(
    inputs,
    outputs,
    lengths,
    labels,
    norm_gain,
    classifier,
    proj_in,
    proj_out,
    query_index,
    prior_fisher,
):
    devices = lax.axis_size("dp")
    own_count, tokens, depth = inputs.shape
    feat_in, feat_out = proj_in.shape[1], proj_out.shape[1]
    width, piece = prior_fisher.shape
    total = own_count * devices
    queries = query_index.shape[0]
    columns = devices // 4
    vmem = pl.BlockSpec(memory_space=pltpu.VMEM)
    smem = pl.BlockSpec(memory_space=pltpu.SMEM)
    hbm = pl.BlockSpec(memory_space=pl.ANY)
    dma = pltpu.SemaphoreType.DMA
    parts = pl.pallas_call(
        functools.partial(solve_kernel, devices),
        out_shape=(
            jax.ShapeDtypeStruct((total, 4 * total), jnp.float32),
            jax.ShapeDtypeStruct((4 * total, piece), jnp.float32),
            jax.ShapeDtypeStruct((8, 4 * total), jnp.float32),
        ),
        in_specs=[smem, smem, vmem, hbm, hbm, hbm, hbm, hbm, hbm],
        out_specs=(vmem, vmem, vmem),
        scratch_shapes=[
            pltpu.VMEM(inputs.shape, jnp.bfloat16),
            pltpu.VMEM(outputs.shape, jnp.bfloat16),
            pltpu.VMEM(classifier.shape[::-1], jnp.bfloat16),
            pltpu.VMEM(proj_in.shape[::-1], jnp.bfloat16),
            pltpu.VMEM(proj_out.shape, jnp.bfloat16),
            pltpu.VMEM((own_count, tokens, 1), jnp.float32),
            pltpu.VMEM((8, depth), jnp.float32),
            pltpu.VMEM((8, depth), jnp.float32),
            pltpu.VMEM((tokens, depth), jnp.bfloat16),
            pltpu.VMEM((total, feat_in, feat_out), jnp.bfloat16),
            pltpu.VMEM((total * feat_in, feat_out), jnp.float32),
            pltpu.VMEM((devices, 4 * total, piece), jnp.bfloat16),
            pltpu.VMEM((devices, piece, piece), jnp.bfloat16),
            pltpu.VMEM((devices, piece, piece), jnp.float32),
            pltpu.VMEM((2, devices, 8, total), jnp.float32),
            dma((columns,)),
            dma((columns,)),
            dma((2 * columns,)),
            dma((devices,)),
            dma((STAGES, columns)),
            dma((STAGES, columns)),
            dma((STAGES, 2 * columns)),
            dma((STAGES, devices)),
            dma((2, devices)),
            dma((2, devices)),
            dma((devices,)),
            dma((5,)),
        ],
        compiler_params=pltpu.CompilerParams(
            collective_id=0, has_side_effects=True, vmem_limit_bytes=56 * 1024 * 1024
        ),
        name="solve",
    )(
        lengths,
        labels,
        norm_gain[None],
        inputs,
        outputs,
        classifier.T,
        proj_in.T,
        proj_out,
        prior_fisher,
    )
    return pl.pallas_call(
        finish_kernel,
        out_shape=(
            jax.ShapeDtypeStruct((piece, queries), jnp.float32),
            jax.ShapeDtypeStruct((own_count, queries), jnp.float32),
        ),
        in_specs=[vmem] * 4,
        out_specs=(vmem, vmem),
        name="finish",
    )(query_index[None], *parts)


def solution(mesh):
    return jax.shard_map(
        body,
        mesh=mesh,
        in_specs=(
            P(("groups", "dp"), None, None),
            P(("groups", "dp"), None, None),
            P(("groups", "dp")),
            P(("groups", "dp")),
            P(),
            P(),
            P(),
            P(),
            P("groups"),
            P("groups", "dp"),
        ),
        out_specs=(P("dp", "groups"), P(("groups", "dp"), None)),
        check_vma=False,
    )
```
